32 devices in a mesh: cluster: 16 (over z, y, x), ens: 2 (over core).
Axes of the slice: x: 2, y: 2, z: 4, core: 2. Of those that a mesh axis runs over, the one named last changes fastest.
Arguments:
- log_rate: float32 [16, 16384], P('ens', 'cluster'), may hold values from -1 to 0.5
- state: float32 [16, 16384], P('ens', 'cluster'), may hold values from -1 to 1
- rate_coef: float32 [16, 16384], P('ens', 'cluster'), may hold values from 0.5 to 2
- state_coef: float32 [16, 16384], P('ens', 'cluster'), may hold values from 0.5 to 2
- near_weight: bfloat16 [3, 16384, 1024], P(None, 'cluster', 'ens'), may hold values from -0.21582031 to 0.21582031
- col_basis: bfloat16 [64, 16384], P(None, 'cluster'), may hold values from -0.1875 to 0.1875
- coupling: float32 [1024, 1024], P('cluster'), may hold values from -0.1875 to 0.1875
- cluster_row_factors: float32 [64, 16384], P(None, 'cluster'), may hold values from -2.25 to 2.25
- ranks: int32 [16], P('cluster'), may hold values from 16 to 64, as said below
Outputs:
- log_rate_next: float32 [16, 16384], P('ens', 'cluster')
- state_next: float32 [16, 16384], P('ens', 'cluster')
The draws below stay inside these ranges and needn't reach their ends.
Inputs may be any that keep to these rules, and one draw needn't show every extreme that they name: `ranks`: each cluster's rank lies in 16 to 64; some cluster has rank 64.
All inputs are finite; a program needn't handle non-finite values.
Results may differ from the reference program's by a relative error of at most 0.0017.
Values may be sent and summed in bfloat16 or wider, within the bound.
A program may use at most 64 MiB of HBM per device.

```python
import math
import jax
import jax.numpy as jnp
from jax import lax

CLUSTER_ROWS = 1024
LARGEST_RANK = 64
CLUSTER_TOTAL = 16
TRIS = 16384
MEMBERS = 16


def draw_ranks(key, part):
    first, second = jax.random.split(key)
    values = jax.random.randint(first, (CLUSTER_TOTAL,), LARGEST_RANK // 4, LARGEST_RANK + 1)
    widest = jax.random.randint(second, (), 0, CLUSTER_TOTAL)
    return values.at[widest].set(LARGEST_RANK).astype(jnp.int32)


def steps_of(rng, dims, cuts, least, top_value):
    def one(axis_at, parts):
        draws = jax.random.uniform(jax.random.fold_in(jax.random.fold_in(rng, 6), axis_at), (parts,), jnp.float32, least / len(cuts), top_value / len(cuts))
        return jnp.repeat(jnp.exp(draws), dims[axis_at] // parts).reshape((-1,) + (1,) * (len(dims) - axis_at - 1))

    gain = one(*cuts[0])
    for cut in cuts[1:]:
        gain = gain * one(*cut)
    return gain


def scatter_about(own_key, extent, deviation, bound, cuts=(), kind=jnp.bfloat16):
    gain = steps_of(own_key, extent, cuts, -0.22, 0.18) if cuts else 1.0
    array = jax.random.normal(own_key, extent, jnp.float32) * deviation * gain
    return jnp.minimum(jnp.maximum(array, -bound), bound).astype(kind)


def setup_inputs(seed: int = 0) -> dict:
    splits = jax.random.split(jax.random.key(seed), 10)
    return {
        "log_rate": jnp.clip(-1.0 + 1.5 * jax.random.uniform(splits[0], (MEMBERS, TRIS), jnp.float32) ** steps_of(splits[0], (MEMBERS, TRIS), ((0, 2), (1, 16)), -0.2, 0.2), -1.0, 0.5),
        "state": jnp.clip(jax.random.uniform(splits[1], (MEMBERS, TRIS), jnp.float32, -1.0, 1.0) * steps_of(splits[1], (MEMBERS, TRIS), ((0, 2), (1, 16)), -0.4, 0.0), -1.0, 1.0),
        "rate_coef": jnp.clip(jnp.exp(math.log(2.0) - 1.3862944 * jax.random.uniform(splits[2], (MEMBERS, TRIS), jnp.float32) ** steps_of(splits[2], (MEMBERS, TRIS), ((0, 2), (1, 16)), -0.2, 0.2)), 0.5, 2.0),
        "state_coef": jnp.clip(jnp.exp(math.log(2.0) - 1.3862944 * jax.random.uniform(splits[3], (MEMBERS, TRIS), jnp.float32) ** steps_of(splits[3], (MEMBERS, TRIS), ((0, 2), (1, 16)), -0.2, 0.2)), 0.5, 2.0),
        "near_weight": scatter_about(splits[4], (3, TRIS, CLUSTER_ROWS), (2.0 / (3 * CLUSTER_ROWS) ** 0.5), 0.21582031, ((1, 16), (2, 2))),
        "col_basis": scatter_about(splits[5], (LARGEST_RANK, TRIS), CLUSTER_ROWS ** -0.5, 0.1875, ((1, 16),)),
        "coupling": scatter_about(splits[6], (CLUSTER_TOTAL * LARGEST_RANK, CLUSTER_TOTAL * LARGEST_RANK), (CLUSTER_TOTAL * LARGEST_RANK) ** -0.5, 0.1875, ((0, 16),), jnp.float32),
        "cluster_row_factors": scatter_about(splits[7], (LARGEST_RANK, TRIS), (3.0 / LARGEST_RANK ** 0.5), 2.25, ((1, 16),), jnp.float32),
        "ranks": draw_ranks(jax.random.fold_in(splits[9], 71), 0),
    }


step_length = 0.5
damping = 0.5


def stress(deficit, near_weight, col_basis, coupling, cluster_row_factors, ranks):
    members = deficit.shape[0]
    grouped = deficit.reshape(members, CLUSTER_TOTAL, CLUSTER_ROWS)
    zero = jnp.zeros((members, 1, CLUSTER_ROWS), deficit.dtype)
    padded = jnp.concatenate([zero, grouped, zero], axis=1)
    windows = jnp.concatenate([padded[:, k:k + CLUSTER_TOTAL] for k in range(3)], axis=2)
    windows = jnp.transpose(windows, (1, 0, 2))
    blocks = jnp.transpose(near_weight.reshape(3, CLUSTER_TOTAL, CLUSTER_ROWS, CLUSTER_ROWS), (1, 2, 0, 3))
    blocks = blocks.reshape(CLUSTER_TOTAL, CLUSTER_ROWS, 3 * CLUSTER_ROWS)

    def one_cluster(item):
        window, block = item
        return jnp.dot(window, block.T, preferred_element_type=jnp.float32)

    near = lax.map(one_cluster, (windows, blocks))
    near = jnp.transpose(near, (1, 0, 2))
    rank_index = jnp.arange(LARGEST_RANK, dtype=jnp.int32)
    coef = jnp.einsum("mjr,kjr->mjk", grouped.astype(jnp.float32),
                      col_basis.reshape(LARGEST_RANK, CLUSTER_TOTAL, CLUSTER_ROWS).astype(jnp.float32),
                      precision=lax.Precision.HIGHEST)
    coef = jnp.where(rank_index[None, None, :] < ranks[None, :, None], coef, 0.0)
    cluster_index = jnp.arange(CLUSTER_TOTAL, dtype=jnp.int32)
    admissible = jnp.abs(cluster_index[:, None] - cluster_index[None, :]) > 1
    blocks_far = jnp.where(admissible[:, None, :, None], coupling.reshape(CLUSTER_TOTAL, LARGEST_RANK, CLUSTER_TOTAL, LARGEST_RANK), 0.0)
    compressed_sum = jnp.einsum("ikjl,mjl->mik", blocks_far, coef, precision=lax.Precision.HIGHEST)
    compressed_sum = jnp.where(rank_index[None, None, :] < ranks[None, :, None], compressed_sum, 0.0)
    distant_part = jnp.einsum("fel,leh->feh", compressed_sum, cluster_row_factors.reshape(LARGEST_RANK, CLUSTER_TOTAL, CLUSTER_ROWS),
                     precision=lax.Precision.HIGHEST)
    return (near + distant_part).reshape(members, CLUSTER_TOTAL * CLUSTER_ROWS)


def rates(current_logarithm, state_now, rate_coef, state_coef, operands):
    rate = jnp.exp(current_logarithm)
    deficit = (rate - 1.0).astype(jnp.bfloat16)
    stress_rate = stress(deficit, *operands)
    state_rate = jnp.exp(-state_now) - rate
    rate_rate = (stress_rate - state_coef * state_rate) / (rate_coef + damping * rate)
    return rate_rate, state_rate


def reference(log_rate, state, rate_coef, state_coef, near_weight, col_basis, coupling, cluster_row_factors, ranks):
    operands = (near_weight, col_basis, coupling, cluster_row_factors, ranks)
    rate_one, state_one = rates(log_rate, state, rate_coef, state_coef, operands)
    rate_two, state_two = rates(log_rate + step_length * rate_one, state + step_length * state_one,
                                rate_coef, state_coef, operands)
    log_rate_next = log_rate + 0.5 * step_length * (rate_one + rate_two)
    state_next = state + 0.5 * step_length * (state_one + state_two)
    return log_rate_next, state_next
```

```python
import functools

import jax
import jax.numpy as jnp
from jax import lax
from jax.experimental import pallas as pl
from jax.experimental.pallas import tpu as pltpu
from jax.sharding import PartitionSpec as P

step_length = 0.5
damping = 0.5

MESH = pl.DeviceIdType.MESH
ROWS = (((1,), (1,)), ((), ()))


def split(value):
    high = value.astype(jnp.bfloat16)
    low = (value - high.astype(jnp.float32)).astype(jnp.bfloat16)
    return high, low


def kernel(
    n,
    log_rate_hbm,
    state_hbm,
    rate_coef_hbm,
    state_coef_hbm,
    near_hbm,
    basis_hbm,
    coupling_hbm,
    factors_hbm,
    ranks_ref,
    log_rate_out,
    state_out,
    log_rate_ref,
    state_ref,
    rate_coef_ref,
    state_coef_ref,
    near_ref,
    basis_ref,
    coupling_ref,
    factors_ref,
    far_in,
    far_out,
    halves,
    halo,
    coef_send,
    coef_recv,
    part_send,
    part_recv,
    load_sem,
    halo_send_sem,
    halo_recv_sem,
    coef_send_sem,
    coef_recv_sem,
    part_send_sem,
    part_recv_sem,
):
    me = lax.axis_index("cluster")
    core = lax.axis_index("ens")
    other = 1 - core
    members, rows = log_rate_ref.shape
    half = rows // 2
    widest = basis_ref.shape[0]

    loads = [
        pltpu.make_async_copy(source, target, load_sem.at[i])
        for i, (source, target) in enumerate(
            (
                (log_rate_hbm, log_rate_ref),
                (basis_hbm, basis_ref),
                (state_hbm, state_ref),
                (coupling_hbm, coupling_ref),
                (factors_hbm, factors_ref),
                (near_hbm, near_ref),
                (rate_coef_hbm, rate_coef_ref),
                (state_coef_hbm, state_coef_ref),
            )
        )
    ]
    for load in loads:
        load.start()

    barrier = pltpu.get_barrier_semaphore()

    def greet(cluster, ens):
        pl.semaphore_signal(barrier, inc=1, device_id=(cluster, ens), device_id_type=MESH)

    for d in range(1, n):
        greet(lax.rem(me + d, n), core)
    greet(me, other)

    @pl.when(me > 0)
    def _():
        greet(me - 1, other)

    @pl.when(me < n - 1)
    def _():
        greet(me + 1, other)

    own_rank = ranks_ref[0]
    lane = lax.broadcasted_iota(jnp.int32, (members, 2 * widest), 1)
    lane_rank = lax.rem(lane, widest)

    zero_coef = jnp.zeros((members, 2 * widest), coef_recv.dtype)
    zero_half = jnp.zeros((members, half), halo.dtype)
    for section in range(2):
        coef_recv[section, me] = zero_coef

        @pl.when(me > 0)
        def _():
            coef_recv[section, jnp.maximum(me - 1, 0)] = zero_coef

        @pl.when(me < n - 1)
        def _():
            coef_recv[section, jnp.minimum(me + 1, n - 1)] = zero_coef

        @pl.when(me == 0)
        def _():
            for slot in range(2):
                halo[section, 0, slot] = zero_half

        @pl.when(me == n - 1)
        def _():
            for slot in range(2):
                halo[section, 2, slot] = zero_half

    def halo_copy(section, k, slot, cluster):
        ens = core if slot == 0 else other
        return pltpu.make_async_remote_copy(
            src_ref=halves.at[section, ens],
            dst_ref=halo.at[section, k, slot],
            send_sem=halo_send_sem.at[section, k, slot],
            recv_sem=halo_recv_sem.at[section, k, slot],
            device_id=(cluster, ens),
            device_id_type=MESH,
        )

    def coef_copy(section, cluster):
        return pltpu.make_async_remote_copy(
            src_ref=coef_send.at[section],
            dst_ref=coef_recv.at[section, me],
            send_sem=coef_send_sem.at[section, cluster],
            recv_sem=coef_recv_sem.at[section, me],
            device_id=(cluster, core),
            device_id_type=MESH,
        )

    def coef_arrival(section, cluster):
        return pltpu.make_async_remote_copy(
            src_ref=coef_send.at[section],
            dst_ref=coef_recv.at[section, cluster],
            send_sem=coef_send_sem.at[section, cluster],
            recv_sem=coef_recv_sem.at[section, cluster],
            device_id=(cluster, core),
            device_id_type=MESH,
        )

    def part_copy(section):
        return pltpu.make_async_remote_copy(
            src_ref=part_send.at[section],
            dst_ref=part_recv.at[section],
            send_sem=part_send_sem.at[section],
            recv_sem=part_recv_sem.at[section],
            device_id=(me, other),
            device_id_type=MESH,
        )

    def each_far(action):
        for d in range(2, n - 1):
            action(lax.rem(me + d, n))

        @pl.when(me == 0)
        def _():
            action(jnp.int32(n - 1))

        @pl.when(me == n - 1)
        def _():
            action(jnp.int32(0))

    def prepare():
        loads[3].wait()
        row = lax.broadcasted_iota(jnp.int32, (widest, 2 * widest), 0)
        kept = row < own_rank
        for j in range(n):
            block = coupling_ref[:, j * widest : (j + 1) * widest]
            block = jnp.concatenate([block, block], axis=1)
            block = jnp.where(jnp.logical_and(kept, jnp.abs(me - j) > 1), block, 0.0)
            high, low = split(block)
            far_in[0:widest, 2 * j * widest : 2 * (j + 1) * widest] = high
            far_in[widest : 2 * widest, 2 * j * widest : 2 * (j + 1) * widest] = low
        loads[4].wait()
        high, low = split(factors_ref[...])
        far_out[0:widest] = high
        far_out[widest : 2 * widest] = high
        far_out[2 * widest : 3 * widest] = low
        far_out[3 * widest : 4 * widest] = low

    def rates(section, current_logarithm):
        rate = jnp.exp(current_logarithm)
        deficit = (rate - 1.0).astype(jnp.bfloat16)
        halves[section, 0] = deficit[:, :half]
        halves[section, 1] = deficit[:, half:]
        halo[section, 1, 0] = halves[section, core]
        basis = basis_ref[...]
        coef = lax.dot_general(
            deficit,
            jnp.concatenate([basis, basis], axis=0),
            ROWS,
            preferred_element_type=jnp.float32,
        )
        coef = jnp.where(lane_rank < own_rank, coef, 0.0)
        high = coef.astype(jnp.bfloat16).astype(jnp.float32)
        coef_send[section] = jnp.where(lane < widest, high, coef - high).astype(jnp.bfloat16)

        if section == 0:
            greeted = n + jnp.where(me > 0, 1, 0) + jnp.where(me < n - 1, 1, 0)
            pl.semaphore_wait(barrier, greeted)

        each_far(lambda cluster: coef_copy(section, cluster).start())

        @pl.when(me > 0)
        def _():
            for slot in range(2):
                halo_copy(section, 2, slot, me - 1).start()

        @pl.when(me < n - 1)
        def _():
            for slot in range(2):
                halo_copy(section, 0, slot, me + 1).start()

        halo_copy(section, 1, 1, me).start()

        if section == 0:
            prepare()
            loads[5].wait()

        def near(k):
            columns = jnp.concatenate([halo[section, k, 0], halo[section, k, 1]], axis=0)
            return lax.dot_general(
                columns, near_ref[k], ROWS, preferred_element_type=jnp.float32
            )

        halo_copy(section, 1, 1, me).wait_recv()
        total = near(1)

        @pl.when(me > 0)
        def _():
            for slot in range(2):
                halo_copy(section, 0, slot, me - 1).wait_recv()

        total = total + near(0)

        @pl.when(me < n - 1)
        def _():
            for slot in range(2):
                halo_copy(section, 2, slot, me + 1).wait_recv()

        total = total + near(2)
        part_send[section] = total[members:]
        part_copy(section).start()

        each_far(lambda cluster: coef_arrival(section, cluster).wait_recv())
        coefs = jnp.concatenate([coef_recv[section, j] for j in range(n)], axis=1)
        reduced = lax.dot_general(coefs, far_in[...], ROWS, preferred_element_type=jnp.float32)
        high, low = split(reduced)
        reduced = jnp.concatenate(
            [jnp.concatenate([high, high], axis=1), jnp.concatenate([low, low], axis=1)], axis=0
        )
        far = jnp.dot(reduced, far_out[...], preferred_element_type=jnp.float32)
        stress_rate = total[:members] + (far[:members] + far[members:])
        part_copy(section).wait_recv()
        return rate, stress_rate + part_recv[section]

    loads[0].wait()
    loads[1].wait()
    log_rate = log_rate_ref[...]
    rate, stress_one = rates(0, log_rate)
    loads[2].wait()
    loads[6].wait()
    loads[7].wait()
    state = state_ref[...]
    rate_coef = rate_coef_ref[...]
    state_coef = state_coef_ref[...]
    state_one = jnp.exp(-state) - rate
    rate_one = (stress_one - state_coef * state_one) / (rate_coef + damping * rate)
    second, stress_two = rates(1, log_rate + step_length * rate_one)
    state_two = jnp.exp(-(state + step_length * state_one)) - second
    rate_two = (stress_two - state_coef * state_two) / (rate_coef + damping * second)
    log_rate_out[...] = log_rate + 0.5 * step_length * (rate_one + rate_two)
    state_out[...] = state + 0.5 * step_length * (state_one + state_two)

    for section in range(2):
        each_far(lambda cluster: coef_copy(section, cluster).wait_send())

        @pl.when(me > 0)
        def _():
            for slot in range(2):
                halo_copy(section, 2, slot, me - 1).wait_send()

        @pl.when(me < n - 1)
        def _():
            for slot in range(2):
                halo_copy(section, 0, slot, me + 1).wait_send()

        halo_copy(section, 1, 1, me).wait_send()
        part_copy(section).wait_send()


def local(n, *args):
    log_rate, near_weight, col_basis, coupling, factors = (args[i] for i in (0, 4, 5, 6, 7))
    members, rows = log_rate.shape
    half = near_weight.shape[2]
    widest = col_basis.shape[0]
    f32, bf16 = jnp.float32, jnp.bfloat16
    anywhere = pl.BlockSpec(memory_space=pl.ANY)
    vmem = pl.BlockSpec(memory_space=pltpu.VMEM)
    return tuple(
        pl.pallas_call(
            functools.partial(kernel, n),
            out_shape=[jax.ShapeDtypeStruct((members, rows), f32)] * 2,
            in_specs=[anywhere] * 8 + [pl.BlockSpec(memory_space=pltpu.SMEM)],
            out_specs=[vmem] * 2,
            scratch_shapes=[
                pltpu.VMEM((members, rows), f32),
                pltpu.VMEM((members, rows), f32),
                pltpu.VMEM((members, rows), f32),
                pltpu.VMEM((members, rows), f32),
                pltpu.VMEM(near_weight.shape, bf16),
                pltpu.VMEM(col_basis.shape, bf16),
                pltpu.VMEM(coupling.shape, f32),
                pltpu.VMEM(factors.shape, f32),
                pltpu.VMEM((2 * widest, n * 2 * widest), bf16),
                pltpu.VMEM((4 * widest, rows), bf16),
                pltpu.VMEM((2, 2, members, half), bf16),
                pltpu.VMEM((2, 3, 2, members, half), bf16),
                pltpu.VMEM((2, members, 2 * widest), bf16),
                pltpu.VMEM((2, n, members, 2 * widest), bf16),
                pltpu.VMEM((2, members, rows), f32),
                pltpu.VMEM((2, members, rows), f32),
                pltpu.SemaphoreType.DMA((8,)),
                pltpu.SemaphoreType.DMA((2, 3, 2)),
                pltpu.SemaphoreType.DMA((2, 3, 2)),
                pltpu.SemaphoreType.DMA((2, n)),
                pltpu.SemaphoreType.DMA((2, n)),
                pltpu.SemaphoreType.DMA((2,)),
                pltpu.SemaphoreType.DMA((2,)),
            ],
            compiler_params=pltpu.CompilerParams(
                collective_id=0, has_side_effects=True, vmem_limit_bytes=60 * 1024 * 1024
            ),
        )(*args)
    )


def solution(mesh):
    in_specs = (
        P("ens", "cluster"),
        P("ens", "cluster"),
        P("ens", "cluster"),
        P("ens", "cluster"),
        P(None, "cluster", "ens"),
        P(None, "cluster"),
        P("cluster", None),
        P(None, "cluster"),
        P("cluster"),
    )
    out_specs = (P("ens", "cluster"), P("ens", "cluster"))
    return jax.shard_map(
        functools.partial(local, mesh.shape["cluster"]),
        mesh=mesh,
        in_specs=in_specs,
        out_specs=out_specs,
        check_vma=False,
    )
```

```python
import functools

import jax
import jax.numpy as jnp
from jax import lax
from jax.experimental import pallas as pl
from jax.experimental.pallas import tpu as pltpu
from jax.sharding import PartitionSpec as P

step_length = 0.5
damping = 0.5

MESH = pl.DeviceIdType.MESH
ROWS = (((1,), (1,)), ((), ()))


def split(value):
    high = value.astype(jnp.bfloat16)
    low = (value - high.astype(jnp.float32)).astype(jnp.bfloat16)
    return high, low


def kernel(
    n,
    log_rate_hbm,
    state_hbm,
    rate_coef_hbm,
    state_coef_hbm,
    near_hbm,
    basis_hbm,
    coupling_hbm,
    factors_hbm,
    ranks_hbm,
    sums_out,
    ranks_ref,
    log_rate_ref,
    state_ref,
    rate_coef_ref,
    state_coef_ref,
    near_ref,
    basis_ref,
    coupling_ref,
    factors_ref,
    far_in,
    far_out,
    halves,
    halo,
    coef_send,
    coef_recv,
    part_send,
    part_recv,
    load_sem,
    halo_send_sem,
    halo_recv_sem,
    coef_send_sem,
    coef_recv_sem,
    part_send_sem,
    part_recv_sem,
):
    me = lax.axis_index("cluster")
    core = lax.axis_index("ens")
    other = 1 - core
    members, rows = log_rate_ref.shape
    half = rows // 2
    widest = basis_ref.shape[0]

    loads = [
        pltpu.make_async_copy(source, target, load_sem.at[i])
        for i, (source, target) in enumerate(
            (
                (log_rate_hbm, log_rate_ref),
                (basis_hbm, basis_ref),
                (state_hbm, state_ref),
                (coupling_hbm, coupling_ref),
                (factors_hbm, factors_ref),
                (near_hbm, near_ref),
                (rate_coef_hbm, rate_coef_ref),
                (state_coef_hbm, state_coef_ref),
                (ranks_hbm, ranks_ref),
            )
        )
    ]
    for i in (0, 1, 8, 2, 3, 4, 5, 6, 7):
        loads[i].start()

    barrier = pltpu.get_barrier_semaphore()

    def greet(cluster, ens):
        pl.semaphore_signal(barrier, inc=1, device_id=(cluster, ens), device_id_type=MESH)

    for d in range(1, n):
        greet(lax.rem(me + d, n), core)
    greet(me, other)

    @pl.when(me > 0)
    def _():
        greet(me - 1, other)

    @pl.when(me < n - 1)
    def _():
        greet(me + 1, other)

    lane = lax.broadcasted_iota(jnp.int32, (members, 2 * widest), 1)
    lane_rank = lax.rem(lane, widest)

    zero_coef = jnp.zeros((members, 2 * widest), coef_recv.dtype)
    zero_half = jnp.zeros((members, half), halo.dtype)
    for section in range(2):
        coef_recv[section, me] = zero_coef

        @pl.when(me > 0)
        def _():
            coef_recv[section, jnp.maximum(me - 1, 0)] = zero_coef

        @pl.when(me < n - 1)
        def _():
            coef_recv[section, jnp.minimum(me + 1, n - 1)] = zero_coef

        @pl.when(me == 0)
        def _():
            for slot in range(2):
                halo[section, 0, slot] = zero_half

        @pl.when(me == n - 1)
        def _():
            for slot in range(2):
                halo[section, 2, slot] = zero_half

    def halo_copy(section, k, slot, cluster):
        ens = core if slot == 0 else other
        return pltpu.make_async_remote_copy(
            src_ref=halves.at[section, ens],
            dst_ref=halo.at[section, k, slot],
            send_sem=halo_send_sem.at[section, k, slot],
            recv_sem=halo_recv_sem.at[section, k, slot],
            device_id=(cluster, ens),
            device_id_type=MESH,
        )

    def coef_copy(section, cluster):
        return pltpu.make_async_remote_copy(
            src_ref=coef_send.at[section],
            dst_ref=coef_recv.at[section, me],
            send_sem=coef_send_sem.at[section, cluster],
            recv_sem=coef_recv_sem.at[section, me],
            device_id=(cluster, core),
            device_id_type=MESH,
        )

    def coef_arrival(section, cluster):
        return pltpu.make_async_remote_copy(
            src_ref=coef_send.at[section],
            dst_ref=coef_recv.at[section, cluster],
            send_sem=coef_send_sem.at[section, cluster],
            recv_sem=coef_recv_sem.at[section, cluster],
            device_id=(cluster, core),
            device_id_type=MESH,
        )

    def part_copy(section):
        return pltpu.make_async_remote_copy(
            src_ref=part_send.at[section],
            dst_ref=part_recv.at[section],
            send_sem=part_send_sem.at[section],
            recv_sem=part_recv_sem.at[section],
            device_id=(me, other),
            device_id_type=MESH,
        )

    def each_far(action):
        for d in sorted(range(2, n - 1), key=lambda d: abs(2 * d - n)):
            action(lax.rem(me + d, n))

        @pl.when(me == 0)
        def _():
            action(jnp.int32(n - 1))

        @pl.when(me == n - 1)
        def _():
            action(jnp.int32(0))

    def prepare(own_rank):
        loads[3].wait()
        row = lax.broadcasted_iota(jnp.int32, (widest, 2 * widest), 0)
        kept = row < own_rank
        for j in range(n):
            block = coupling_ref[:, j * widest : (j + 1) * widest]
            block = jnp.concatenate([block, block], axis=1)
            block = jnp.where(jnp.logical_and(kept, jnp.abs(me - j) > 1), block, 0.0)
            high, low = split(block)
            far_in[0:widest, 2 * j * widest : 2 * (j + 1) * widest] = high
            far_in[widest : 2 * widest, 2 * j * widest : 2 * (j + 1) * widest] = low
        loads[4].wait()
        high, low = split(factors_ref[...])
        far_out[0:widest] = high
        far_out[widest : 2 * widest] = high
        far_out[2 * widest : 3 * widest] = low
        far_out[3 * widest : 4 * widest] = low

    def rates(section, current_logarithm, own_rank):
        rate = jnp.exp(current_logarithm)
        deficit = (rate - 1.0).astype(jnp.bfloat16)
        halves[section, 0] = deficit[:, :half]
        halves[section, 1] = deficit[:, half:]
        halo[section, 1, 0] = halves[section, core]
        basis = basis_ref[...]
        coef = lax.dot_general(
            deficit,
            jnp.concatenate([basis, basis], axis=0),
            ROWS,
            preferred_element_type=jnp.float32,
        )
        coef = jnp.where(lane_rank < own_rank, coef, 0.0)
        high = coef.astype(jnp.bfloat16).astype(jnp.float32)
        coef_send[section] = jnp.where(lane < widest, high, coef - high).astype(jnp.bfloat16)

        if section == 0:
            greeted = n + jnp.where(me > 0, 1, 0) + jnp.where(me < n - 1, 1, 0)
            pl.semaphore_wait(barrier, greeted)

        each_far(lambda cluster: coef_copy(section, cluster).start())

        @pl.when(me > 0)
        def _():
            for slot in range(2):
                halo_copy(section, 2, slot, me - 1).start()

        @pl.when(me < n - 1)
        def _():
            for slot in range(2):
                halo_copy(section, 0, slot, me + 1).start()

        halo_copy(section, 1, 1, me).start()

        if section == 0:
            prepare(own_rank)
            loads[5].wait()

        def near(k):
            columns = jnp.concatenate([halo[section, k, 0], halo[section, k, 1]], axis=0)
            return lax.dot_general(
                columns, near_ref[k], ROWS, preferred_element_type=jnp.float32
            )

        halo_copy(section, 1, 1, me).wait_recv()
        total = near(1)

        @pl.when(me > 0)
        def _():
            for slot in range(2):
                halo_copy(section, 0, slot, me - 1).wait_recv()

        total = total + near(0)

        @pl.when(me < n - 1)
        def _():
            for slot in range(2):
                halo_copy(section, 2, slot, me + 1).wait_recv()

        total = total + near(2)
        part_send[section] = total[members:]
        part_copy(section).start()

        each_far(lambda cluster: coef_arrival(section, cluster).wait_recv())
        coefs = jnp.concatenate([coef_recv[section, j] for j in range(n)], axis=1)
        reduced = lax.dot_general(coefs, far_in[...], ROWS, preferred_element_type=jnp.float32)
        high, low = split(reduced)
        reduced = jnp.concatenate(
            [jnp.concatenate([high, high], axis=1), jnp.concatenate([low, low], axis=1)], axis=0
        )
        far = jnp.dot(reduced, far_out[...], preferred_element_type=jnp.float32)
        stress_rate = total[:members] + (far[:members] + far[members:])
        part_copy(section).wait_recv()
        return rate, stress_rate + part_recv[section]

    loads[0].wait()
    loads[1].wait()
    loads[8].wait()
    own_rank = ranks_ref[0]
    log_rate = log_rate_ref[...]
    rate, stress_one = rates(0, log_rate, own_rank)
    loads[2].wait()
    loads[6].wait()
    loads[7].wait()
    state = state_ref[...]
    rate_coef = rate_coef_ref[...]
    state_coef = state_coef_ref[...]
    state_one = jnp.exp(-state) - rate
    rate_one = (stress_one - state_coef * state_one) / (rate_coef + damping * rate)
    second, stress_two = rates(1, log_rate + step_length * rate_one, own_rank)
    state_two = jnp.exp(-(state + step_length * state_one)) - second
    rate_two = (stress_two - state_coef * state_two) / (rate_coef + damping * second)
    sums_out[0] = rate_one + rate_two
    sums_out[1] = state_one + state_two

    for section in range(2):
        each_far(lambda cluster: coef_copy(section, cluster).wait_send())

        @pl.when(me > 0)
        def _():
            for slot in range(2):
                halo_copy(section, 2, slot, me - 1).wait_send()

        @pl.when(me < n - 1)
        def _():
            for slot in range(2):
                halo_copy(section, 0, slot, me + 1).wait_send()

        halo_copy(section, 1, 1, me).wait_send()
        part_copy(section).wait_send()


def finish(sums_ref, log_rate_ref, state_ref, log_rate_out, state_out):
    log_rate_out[...] = log_rate_ref[...] + 0.5 * step_length * sums_ref[0]
    state_out[...] = state_ref[...] + 0.5 * step_length * sums_ref[1]


def local(n, *args):
    log_rate, near_weight, col_basis, coupling, factors = (args[i] for i in (0, 4, 5, 6, 7))
    members, rows = log_rate.shape
    half = near_weight.shape[2]
    widest = col_basis.shape[0]
    f32, bf16 = jnp.float32, jnp.bfloat16
    in_hbm = pl.BlockSpec(memory_space=pltpu.HBM)
    vmem = pl.BlockSpec(memory_space=pltpu.VMEM)
    sums = pl.pallas_call(
            functools.partial(kernel, n),
            out_shape=pltpu.VMEM((2, members, rows), f32),
            in_specs=[in_hbm] * 9,
            out_specs=vmem,
            scratch_shapes=[
                pltpu.SMEM((1,), jnp.int32),
                pltpu.VMEM((members, rows), f32),
                pltpu.VMEM((members, rows), f32),
                pltpu.VMEM((members, rows), f32),
                pltpu.VMEM((members, rows), f32),
                pltpu.VMEM(near_weight.shape, bf16),
                pltpu.VMEM(col_basis.shape, bf16),
                pltpu.VMEM(coupling.shape, f32),
                pltpu.VMEM(factors.shape, f32),
                pltpu.VMEM((2 * widest, n * 2 * widest), bf16),
                pltpu.VMEM((4 * widest, rows), bf16),
                pltpu.VMEM((2, 2, members, half), bf16),
                pltpu.VMEM((2, 3, 2, members, half), bf16),
                pltpu.VMEM((2, members, 2 * widest), bf16),
                pltpu.VMEM((2, n, members, 2 * widest), bf16),
                pltpu.VMEM((2, members, rows), f32),
                pltpu.VMEM((2, members, rows), f32),
                pltpu.SemaphoreType.DMA((9,)),
                pltpu.SemaphoreType.DMA((2, 3, 2)),
                pltpu.SemaphoreType.DMA((2, 3, 2)),
                pltpu.SemaphoreType.DMA((2, n)),
                pltpu.SemaphoreType.DMA((2, n)),
                pltpu.SemaphoreType.DMA((2,)),
                pltpu.SemaphoreType.DMA((2,)),
            ],
            compiler_params=pltpu.CompilerParams(
                collective_id=0, has_side_effects=True, vmem_limit_bytes=60 * 1024 * 1024
            ),
        )(*args)
    return tuple(
        pl.pallas_call(
            finish,
            out_shape=[jax.ShapeDtypeStruct((members, rows), f32)] * 2,
            in_specs=[vmem] * 3,
            out_specs=[vmem] * 2,
            compiler_params=pltpu.CompilerParams(vmem_limit_bytes=1024 * 1024),
        )(sums, args[0], args[1])
    )


def solution(mesh):
    in_specs = (
        P("ens", "cluster"),
        P("ens", "cluster"),
        P("ens", "cluster"),
        P("ens", "cluster"),
        P(None, "cluster", "ens"),
        P(None, "cluster"),
        P("cluster", None),
        P(None, "cluster"),
        P("cluster"),
    )
    out_specs = (P("ens", "cluster"), P("ens", "cluster"))
    return jax.shard_map(
        functools.partial(local, mesh.shape["cluster"]),
        mesh=mesh,
        in_specs=in_specs,
        out_specs=out_specs,
        check_vma=False,
    )
```

```python
import functools

import jax
import jax.numpy as jnp
from jax import lax
from jax.experimental import pallas as pl
from jax.experimental.pallas import tpu as pltpu
from jax.sharding import PartitionSpec as P

step_length = 0.5
damping = 0.5

MESH = pl.DeviceIdType.MESH
ROWS = (((1,), (1,)), ((), ()))


def split(value):
    high = value.astype(jnp.bfloat16)
    low = (value - high.astype(jnp.float32)).astype(jnp.bfloat16)
    return high, low


def kernel(
    n,
    log_rate_hbm,
    state_hbm,
    rate_coef_hbm,
    state_coef_hbm,
    near_hbm,
    basis_hbm,
    coupling_hbm,
    factors_hbm,
    ranks_hbm,
    sums_out,
    ranks_ref,
    log_rate_ref,
    state_ref,
    rate_coef_ref,
    state_coef_ref,
    near_ref,
    basis_ref,
    coupling_ref,
    factors_ref,
    far_in,
    far_out,
    halves,
    halo,
    coef_send,
    coef_recv,
    part_send,
    part_recv,
    load_sem,
    halo_send_sem,
    halo_recv_sem,
    coef_send_sem,
    coef_recv_sem,
    relay_send_sem,
    part_send_sem,
    part_recv_sem,
):
    me = lax.axis_index("cluster")
    core = lax.axis_index("ens")
    other = 1 - core
    members, rows = log_rate_ref.shape
    half = rows // 2
    widest = basis_ref.shape[0]

    loads = [
        pltpu.make_async_copy(source, target, load_sem.at[i])
        for i, (source, target) in enumerate(
            (
                (log_rate_hbm, log_rate_ref),
                (basis_hbm, basis_ref),
                (state_hbm, state_ref),
                (coupling_hbm, coupling_ref),
                (factors_hbm, factors_ref),
                (near_hbm, near_ref),
                (rate_coef_hbm, rate_coef_ref),
                (state_coef_hbm, state_coef_ref),
                (ranks_hbm, ranks_ref),
            )
        )
    ]
    for i in (0, 1, 8, 2, 3, 4, 5, 6, 7):
        loads[i].start()

    barrier = pltpu.get_barrier_semaphore()

    def greet(cluster, ens):
        pl.semaphore_signal(barrier, inc=1, device_id=(cluster, ens), device_id_type=MESH)

    plane = 4 if n % 4 == 0 and n > 4 else n
    planes = n // plane
    place, level = lax.rem(me, plane), lax.div(me, plane)

    def at(turn, up):
        if plane == n:
            return lax.rem(me + turn, n)
        places = (
            place,
            place + 1 - 2 * lax.rem(place, 2),
            place + 2 - 4 * lax.div(place, 2),
            3 - place,
        )
        return lax.rem(level + up, planes) * plane + places[turn]

    beside = {1, planes - 1}
    inner = sorted(range(1, plane), reverse=True)
    direct = [(turn, 0) for turn in inner]
    relays = []
    if planes > 1:
        ups = sorted(range(1, planes), key=lambda up: abs(2 * up - planes))
        direct += [(0, up) for up in ups]
        direct += [(turn, up) for turn in (1, 2) for up in ups if up in beside]
        relays = [(3, up) for up in ups]
        relays += [(turn, up) for turn in (1, 2) for up in ups if up not in beside]

    for turn, up in direct:
        greet(at(turn, up), core)
    greet(me, other)
    greeted = len(direct) + 1

    starts = jnp.logical_and(me > 0, place == 0)
    ends = jnp.logical_and(me < n - 1, place == plane - 1)
    pairs = ((me > 0, me - 1, other), (me < n - 1, me + 1, other))
    if planes > 1:
        pairs += ((starts, me - 1, core), (ends, me + 1, core))
    for there, cluster, ens in pairs:
        greeted = greeted + jnp.where(there, 1, 0)

        @pl.when(there)
        def _():
            greet(cluster, ens)

    lane = lax.broadcasted_iota(jnp.int32, (members, 2 * widest), 1)
    lane_rank = lax.rem(lane, widest)

    zero_coef = jnp.zeros((members, 2 * widest), coef_recv.dtype)
    zero_half = jnp.zeros((members, half), halo.dtype)
    for section in range(2):
        coef_recv[section, me] = zero_coef
        if section == 1:

            @pl.when(me > 0)
            def _():
                coef_recv[section, jnp.maximum(me - 1, 0)] = zero_coef

            @pl.when(me < n - 1)
            def _():
                coef_recv[section, jnp.minimum(me + 1, n - 1)] = zero_coef

        @pl.when(me == 0)
        def _():
            for slot in range(2):
                halo[section, 0, slot] = zero_half

        @pl.when(me == n - 1)
        def _():
            for slot in range(2):
                halo[section, 2, slot] = zero_half

    def halo_copy(section, k, slot, cluster):
        ens = core if slot == 0 else other
        return pltpu.make_async_remote_copy(
            src_ref=halves.at[section, ens],
            dst_ref=halo.at[section, k, slot],
            send_sem=halo_send_sem.at[section, k, slot],
            recv_sem=halo_recv_sem.at[section, k, slot],
            device_id=(cluster, ens),
            device_id_type=MESH,
        )

    def coef_copy(section, cluster):
        return pltpu.make_async_remote_copy(
            src_ref=coef_send.at[section],
            dst_ref=coef_recv.at[section, me],
            send_sem=coef_send_sem.at[section, cluster],
            recv_sem=coef_recv_sem.at[section, me],
            device_id=(cluster, core),
            device_id_type=MESH,
        )

    def coef_arrival(section, cluster):
        return pltpu.make_async_remote_copy(
            src_ref=coef_send.at[section],
            dst_ref=coef_recv.at[section, cluster],
            send_sem=coef_send_sem.at[section, cluster],
            recv_sem=coef_recv_sem.at[section, cluster],
            device_id=(cluster, core),
            device_id_type=MESH,
        )

    def relay_copy(at_relay):
        turn, up = relays[at_relay]
        source = at(turn, 0)
        return pltpu.make_async_remote_copy(
            src_ref=coef_recv.at[0, source],
            dst_ref=coef_recv.at[0, source],
            send_sem=relay_send_sem.at[at_relay],
            recv_sem=coef_recv_sem.at[0, source],
            device_id=(at(0, up), core),
            device_id_type=MESH,
        )

    def each_direct(action):
        for turn, up in direct:
            action(at(turn, up))

    def part_copy(section):
        return pltpu.make_async_remote_copy(
            src_ref=part_send.at[section],
            dst_ref=part_recv.at[section],
            send_sem=part_send_sem.at[section],
            recv_sem=part_recv_sem.at[section],
            device_id=(me, other),
            device_id_type=MESH,
        )

    def each_far(action):
        for d in sorted(range(2, n - 1), key=lambda d: abs(2 * d - n)):
            action(lax.rem(me + d, n))

        @pl.when(me == 0)
        def _():
            action(jnp.int32(n - 1))

        @pl.when(me == n - 1)
        def _():
            action(jnp.int32(0))

    def prepare(own_rank):
        loads[3].wait()
        row = lax.broadcasted_iota(jnp.int32, (widest, 2 * widest), 0)
        kept = row < own_rank
        for j in range(n):
            block = coupling_ref[:, j * widest : (j + 1) * widest]
            block = jnp.concatenate([block, block], axis=1)
            block = jnp.where(jnp.logical_and(kept, jnp.abs(me - j) > 1), block, 0.0)
            high, low = split(block)
            far_in[0:widest, 2 * j * widest : 2 * (j + 1) * widest] = high
            far_in[widest : 2 * widest, 2 * j * widest : 2 * (j + 1) * widest] = low
        loads[4].wait()
        high, low = split(factors_ref[...])
        far_out[0:widest] = high
        far_out[widest : 2 * widest] = high
        far_out[2 * widest : 3 * widest] = low
        far_out[3 * widest : 4 * widest] = low

    def rates(section, current_logarithm, own_rank):
        rate = jnp.exp(current_logarithm)
        deficit = (rate - 1.0).astype(jnp.bfloat16)
        halves[section, 0] = deficit[:, :half]
        halves[section, 1] = deficit[:, half:]
        halo[section, 1, 0] = halves[section, core]
        basis = basis_ref[...]
        coef = lax.dot_general(
            deficit,
            jnp.concatenate([basis, basis], axis=0),
            ROWS,
            preferred_element_type=jnp.float32,
        )
        coef = jnp.where(lane_rank < own_rank, coef, 0.0)
        high = coef.astype(jnp.bfloat16).astype(jnp.float32)
        coef_send[section] = jnp.where(lane < widest, high, coef - high).astype(jnp.bfloat16)

        if section == 0:
            pl.semaphore_wait(barrier, greeted)
            each_direct(lambda cluster: coef_copy(section, cluster).start())
        else:
            each_far(lambda cluster: coef_copy(section, cluster).start())

        @pl.when(me > 0)
        def _():
            for slot in range(2):
                halo_copy(section, 2, slot, me - 1).start()

        @pl.when(me < n - 1)
        def _():
            for slot in range(2):
                halo_copy(section, 0, slot, me + 1).start()

        halo_copy(section, 1, 1, me).start()

        if section == 0:
            prepare(own_rank)
            loads[5].wait()

        def near(k):
            columns = jnp.concatenate([halo[section, k, 0], halo[section, k, 1]], axis=0)
            return lax.dot_general(
                columns, near_ref[k], ROWS, preferred_element_type=jnp.float32
            )

        halo_copy(section, 1, 1, me).wait_recv()
        total = near(1)

        if section == 0:
            for turn in inner:
                coef_arrival(section, at(turn, 0)).wait_recv()
                for i, (relayed, _) in enumerate(relays):
                    if relayed == turn:
                        relay_copy(i).start()

        @pl.when(me > 0)
        def _():
            for slot in range(2):
                halo_copy(section, 0, slot, me - 1).wait_recv()

        total = total + near(0)

        @pl.when(me < n - 1)
        def _():
            for slot in range(2):
                halo_copy(section, 2, slot, me + 1).wait_recv()

        total = total + near(2)
        part_send[section] = total[members:]
        part_copy(section).start()

        if section == 0:
            for turn in range(min(plane, 4) if planes > 1 else 0):
                for up in range(1, planes):
                    coef_arrival(section, at(turn, up)).wait_recv()
        else:
            each_far(lambda cluster: coef_arrival(section, cluster).wait_recv())
        coefs = jnp.concatenate([coef_recv[section, j] for j in range(n)], axis=1)
        reduced = lax.dot_general(coefs, far_in[...], ROWS, preferred_element_type=jnp.float32)
        high, low = split(reduced)
        reduced = jnp.concatenate(
            [jnp.concatenate([high, high], axis=1), jnp.concatenate([low, low], axis=1)], axis=0
        )
        far = jnp.dot(reduced, far_out[...], preferred_element_type=jnp.float32)
        stress_rate = total[:members] + (far[:members] + far[members:])
        part_copy(section).wait_recv()
        return rate, stress_rate + part_recv[section]

    loads[0].wait()
    loads[1].wait()
    loads[8].wait()
    own_rank = ranks_ref[0]
    log_rate = log_rate_ref[...]
    rate, stress_one = rates(0, log_rate, own_rank)
    loads[2].wait()
    loads[6].wait()
    loads[7].wait()
    state = state_ref[...]
    rate_coef = rate_coef_ref[...]
    state_coef = state_coef_ref[...]
    state_one = jnp.exp(-state) - rate
    rate_one = (stress_one - state_coef * state_one) / (rate_coef + damping * rate)
    second, stress_two = rates(1, log_rate + step_length * rate_one, own_rank)
    state_two = jnp.exp(-(state + step_length * state_one)) - second
    rate_two = (stress_two - state_coef * state_two) / (rate_coef + damping * second)
    sums_out[0] = rate_one + rate_two
    sums_out[1] = state_one + state_two

    for section in range(2):
        if section == 0:
            each_direct(lambda cluster: coef_copy(section, cluster).wait_send())
            for i in range(len(relays)):
                relay_copy(i).wait_send()
        else:
            each_far(lambda cluster: coef_copy(section, cluster).wait_send())

        @pl.when(me > 0)
        def _():
            for slot in range(2):
                halo_copy(section, 2, slot, me - 1).wait_send()

        @pl.when(me < n - 1)
        def _():
            for slot in range(2):
                halo_copy(section, 0, slot, me + 1).wait_send()

        halo_copy(section, 1, 1, me).wait_send()
        part_copy(section).wait_send()


def finish(sums_ref, log_rate_ref, state_ref, log_rate_out, state_out):
    log_rate_out[...] = log_rate_ref[...] + 0.5 * step_length * sums_ref[0]
    state_out[...] = state_ref[...] + 0.5 * step_length * sums_ref[1]


def local(n, *args):
    log_rate, near_weight, col_basis, coupling, factors = (args[i] for i in (0, 4, 5, 6, 7))
    members, rows = log_rate.shape
    half = near_weight.shape[2]
    widest = col_basis.shape[0]
    f32, bf16 = jnp.float32, jnp.bfloat16
    in_hbm = pl.BlockSpec(memory_space=pltpu.HBM)
    vmem = pl.BlockSpec(memory_space=pltpu.VMEM)
    sums = pl.pallas_call(
            functools.partial(kernel, n),
            out_shape=pltpu.VMEM((2, members, rows), f32),
            in_specs=[in_hbm] * 9,
            out_specs=vmem,
            scratch_shapes=[
                pltpu.SMEM((1,), jnp.int32),
                pltpu.VMEM((members, rows), f32),
                pltpu.VMEM((members, rows), f32),
                pltpu.VMEM((members, rows), f32),
                pltpu.VMEM((members, rows), f32),
                pltpu.VMEM(near_weight.shape, bf16),
                pltpu.VMEM(col_basis.shape, bf16),
                pltpu.VMEM(coupling.shape, f32),
                pltpu.VMEM(factors.shape, f32),
                pltpu.VMEM((2 * widest, n * 2 * widest), bf16),
                pltpu.VMEM((4 * widest, rows), bf16),
                pltpu.VMEM((2, 2, members, half), bf16),
                pltpu.VMEM((2, 3, 2, members, half), bf16),
                pltpu.VMEM((2, members, 2 * widest), bf16),
                pltpu.VMEM((2, n, members, 2 * widest), bf16),
                pltpu.VMEM((2, members, rows), f32),
                pltpu.VMEM((2, members, rows), f32),
                pltpu.SemaphoreType.DMA((9,)),
                pltpu.SemaphoreType.DMA((2, 3, 2)),
                pltpu.SemaphoreType.DMA((2, 3, 2)),
                pltpu.SemaphoreType.DMA((2, n)),
                pltpu.SemaphoreType.DMA((2, n)),
                pltpu.SemaphoreType.DMA((n,)),
                pltpu.SemaphoreType.DMA((2,)),
                pltpu.SemaphoreType.DMA((2,)),
            ],
            compiler_params=pltpu.CompilerParams(
                collective_id=0, has_side_effects=True, vmem_limit_bytes=60 * 1024 * 1024
            ),
        )(*args)
    return tuple(
        pl.pallas_call(
            finish,
            out_shape=[jax.ShapeDtypeStruct((members, rows), f32)] * 2,
            in_specs=[vmem] * 3,
            out_specs=[vmem] * 2,
            compiler_params=pltpu.CompilerParams(vmem_limit_bytes=1024 * 1024),
        )(sums, args[0], args[1])
    )


def solution(mesh):
    in_specs = (
        P("ens", "cluster"),
        P("ens", "cluster"),
        P("ens", "cluster"),
        P("ens", "cluster"),
        P(None, "cluster", "ens"),
        P(None, "cluster"),
        P("cluster", None),
        P(None, "cluster"),
        P("cluster"),
    )
    out_specs = (P("ens", "cluster"), P("ens", "cluster"))
    return jax.shard_map(
        functools.partial(local, mesh.shape["cluster"]),
        mesh=mesh,
        in_specs=in_specs,
        out_specs=out_specs,
        check_vma=False,
    )
```
